512 devices in a mesh: wl: 16 (over y, core), sec: 32 (over x, z).
Axes of the slice: x: 4, y: 8, z: 8, core: 2. Of those that a mesh axis runs over, the one named last changes fastest.
Arguments:
- sections: float32 [128, 32, 2, 2, 128, 128], P('sec', None, None, None, 'wl'), as said below
- launch_mode: int32 [32], P('wl'), may hold values from 0 to 127
Outputs:
- forward_field: float32 [128, 32, 2, 128], P('sec', 'wl')
- backward_field: float32 [128, 32, 2, 128], P('sec', 'wl')
The draws below stay inside these ranges and needn't reach their ends.
Inputs may be any that keep to these rules, and one draw needn't show every extreme that they name: `sections`: every entry is finite; each matrix is a unit-modulus diagonal plus a full coupling, scaled so that it keeps a field's power on average.
All inputs are finite; a program needn't handle non-finite values.
Results may differ from the reference program's by a relative error of at most 0.0003.
Values sent between devices are 32-bit elements; how exact they have to be, the bound alone decides.
No kernel may reach another device: no remote copies, remote signals or barrier semaphores. Data moves between devices by JAX's collectives and lax.ppermute only.
A program may use at most 64 MiB of HBM per device.

```python
import math
import jax
import jax.numpy as jnp
from jax import lax

M = 128
SECTIONS = 128
NW = 32


def draw_sections(key, part):
    key_phase, key_couple = jax.random.split(jax.random.fold_in(key, 17))
    phases = jax.random.uniform(key_phase, (SECTIONS, NW, 2, M), jnp.float32, -math.pi, math.pi)
    strength = 0.35
    coupling = jax.random.normal(key_couple, (SECTIONS, NW, 2, 2, M, M), jnp.float32) * (strength / math.sqrt(2.0 * M))
    unit_matrix = jnp.eye(M, dtype=jnp.float32)
    real_part = jnp.cos(phases)[..., None] * unit_matrix
    imag_part = jnp.sin(phases)[..., None] * unit_matrix
    matrices = (jnp.stack([real_part, imag_part], axis=3) + coupling) / math.sqrt(1.0 + strength * strength)
    return matrices.astype(jnp.float32)


def touch_ends(entries, rng, low, largest):
    shape = entries.shape
    place = [jax.random.randint(jax.random.fold_in(rng, axis), (), 0, shape[axis]) for axis in range(len(shape))]
    entries = entries.at[tuple(place)].set(low)
    longest = shape.index(max(shape))
    place[longest] = (place[longest] + 1) % shape[longest]
    return entries.at[tuple(place)].set(largest)


def setup_inputs(seed: int = 0) -> dict:
    splits = jax.random.split(jax.random.key(seed), 3)
    sections = draw_sections(jax.random.fold_in(splits[2], 71), 0)
    launch_mode = touch_ends(jax.random.randint(splits[1], (NW,), 0, M), jax.random.fold_in(splits[1], 1), 0, M - 1).astype(jnp.int32)
    return dict(sections=sections, launch_mode=launch_mode)


def complex_apply(matrix, vector):
    real_part = jnp.einsum('wij,wj->wi', matrix[:, 0], vector[:, 0], precision=lax.Precision.HIGHEST) - jnp.einsum('wij,wj->wi', matrix[:, 1], vector[:, 1], precision=lax.Precision.HIGHEST)
    imag_part = jnp.einsum('wij,wj->wi', matrix[:, 0], vector[:, 1], precision=lax.Precision.HIGHEST) + jnp.einsum('wij,wj->wi', matrix[:, 1], vector[:, 0], precision=lax.Precision.HIGHEST)
    return jnp.stack([real_part, imag_part], axis=1)

def reference(sections, launch_mode):
    onehot = (jnp.arange(M)[None, :] == launch_mode[:, None]).astype(jnp.float32) * math.sqrt(M)
    launch_field = jnp.stack([onehot, jnp.zeros_like(onehot)], axis=1)

    def forward_step(field, matrix):
        nxt_field = complex_apply(matrix, field)
        return (nxt_field, nxt_field)
    final_forward, forward_field = lax.scan(forward_step, launch_field, sections[:, :, 0])

    def backward_step(field, matrix):
        return (complex_apply(matrix, field), field)
    final_backward, backward_field = lax.scan(backward_step, launch_field, sections[:, :, 1], reverse=True)
    return (forward_field, backward_field)
```

```python
import functools
import math

import jax
import jax.numpy as jnp
from jax import lax
from jax.experimental import pallas as pl
from jax.experimental.pallas import tpu as pltpu
from jax.sharding import Mesh, PartitionSpec as P

M = 128
F32 = jnp.float32
BF16 = jnp.bfloat16
VMEM_SPEC = pl.BlockSpec(memory_space=pltpu.VMEM)
SMEM_SPEC = pl.BlockSpec(memory_space=pltpu.SMEM)
HBM_SPEC = pl.BlockSpec(memory_space=pltpu.HBM)
PARAMS = pltpu.CompilerParams(vmem_limit_bytes=24 * 1024 * 1024)


def slot_of(zh, zl):
    return jnp.where(zh == 0, zl, 3 - zl)


def place():
    x, zh, zl = lax.axis_index("x"), lax.axis_index("zh"), lax.axis_index("zl")
    slot = slot_of(zh, zl)
    direction = lax.rem(slot, 2)
    spot = 2 * x + zh
    spot = jnp.where(direction == 0, spot, 7 - spot)
    return slot // 2, direction, lax.rem(spot, 4), spot // 4


def gather_kernel(sections, out, sem):
    zh = lax.axis_index("zh")
    copies = []
    for zl in range(4):
        slot = slot_of(zh, zl)
        for c in range(4):
            copy = pltpu.make_async_copy(sections.at[c, :, slot], out.at[:, zl, c], sem.at[zl, c])
            copy.start()
            copies.append(copy)
    for copy in copies:
        copy.wait()


def split(value):
    high = value.astype(BF16)
    return high, (value - high.astype(F32)).astype(BF16)


def as_left(mat):
    high, low = split(jnp.concatenate(mat, axis=1))
    return jnp.concatenate([high, low], axis=0), high


def as_right(mat):
    real, imag = mat
    real_high, real_low = split(real)
    imag_high, imag_low = split(imag)
    high = jnp.concatenate(
        [
            jnp.concatenate([real_high, imag_high], axis=1),
            jnp.concatenate([-imag_high, real_high], axis=1),
        ],
        axis=0,
    )
    low = jnp.concatenate(
        [
            jnp.concatenate([real_low, imag_low], axis=1),
            jnp.concatenate([-imag_low, real_low], axis=1),
        ],
        axis=0,
    )
    return high, low


def product(outer_mat, inner_mat):
    both, high = as_left(outer_mat)
    right_high, right_low = as_right(inner_mat)
    wide = jnp.dot(both, right_high, preferred_element_type=F32)
    more = jnp.dot(high, right_low, preferred_element_type=F32)
    total = wide[:M] + (wide[M:] + more)
    return total[:, :M], total[:, M:]


def section_of(recv, order, step):
    index = jnp.where(order == 0, step, 15 - step)
    zl, c = index // 4, lax.rem(index, 4)
    return tuple(recv[:, zl, c, part].reshape(M, M) for part in range(2))


def tree_kernel(recv, total, keep):
    _, direction, _, _ = place()
    level = [section_of(recv, direction, step) for step in range(16)]
    kept = 0
    while len(level) > 1:
        level = [product(level[2 * k + 1], level[2 * k]) for k in range(len(level) // 2)]
        if len(level) > 1:
            for k in range(0, len(level), 2):
                for part in range(2):
                    keep[kept, part] = level[k][part]
                kept += 1
    for part in range(2):
        total[part] = level[0][part]


def matvec(mat, vec, eye):
    mat_real, mat_imag = mat
    real, imag = vec
    out_real = jnp.sum(mat_real * real - mat_imag * imag, axis=1, keepdims=True)
    out_imag = jnp.sum(mat_real * imag + mat_imag * real, axis=1, keepdims=True)
    return (
        jnp.sum(jnp.where(eye, out_real, 0.0), axis=0, keepdims=True),
        jnp.sum(jnp.where(eye, out_imag, 0.0), axis=0, keepdims=True),
    )


def diagonal():
    return lax.broadcasted_iota(jnp.int32, (M, M), 0) == lax.broadcasted_iota(jnp.int32, (M, M), 1)


def launch_vector(mode, b):
    lane = lax.broadcasted_iota(jnp.int32, (1, M), 1)
    onehot = jnp.where(lane == mode[b], jnp.float32(math.sqrt(M)), 0.0)
    return onehot, jnp.zeros_like(onehot)


def middle_kernel(mode, own, near, beside, across, middle, mats):
    b, _, spot, _ = place()
    for s, ref in enumerate((own, near, beside, across)):
        mats[s] = ref[...]
    eye = diagonal()
    vec = launch_vector(mode, b)
    for step in range(4):
        which = spot ^ step
        vec = matvec((mats[which, 0], mats[which, 1]), vec, eye)
    middle[0:1] = vec[0]
    middle[1:2] = vec[1]
    middle[2:8] = jnp.zeros((6, M), F32)


def fields_kernel(mode, own, near, beside, across, middle, recv, keep, out, mats):
    b, direction, spot, upper = place()
    for s, ref in enumerate((own, near, beside, across)):
        mats[s] = ref[...]
    eye = diagonal()
    launch = launch_vector(mode, b)
    start = tuple(jnp.where(upper == 1, middle[part : part + 1], launch[part]) for part in range(2))

    def enter(step, vec):
        which = spot ^ step
        return matvec((mats[which, 0], mats[which, 1]), vec, eye)

    states = [None] * 17
    states[0] = lax.fori_loop(0, spot, enter, start)

    def kept(k):
        return keep[k, 0], keep[k, 1]

    states[16] = matvec((own[0], own[1]), states[0], eye)
    states[8] = matvec(kept(6), states[0], eye)
    for k in range(2):
        states[8 * k + 4] = matvec(kept(4 + k), states[8 * k], eye)
    for k in range(4):
        states[4 * k + 2] = matvec(kept(k), states[4 * k], eye)
    for k in range(8):
        states[2 * k + 1] = matvec(section_of(recv, direction, 2 * k), states[2 * k], eye)
    for index in range(16):
        for part in range(2):
            out[index // 4, 2 * (index % 4) + part : 2 * (index % 4) + part + 1] = jnp.where(
                direction == 0, states[index + 1][part], states[15 - index][part]
            )


def output_kernel(returned, forward, backward):
    zh = lax.axis_index("zh")
    for b in range(2):
        for d, ref in enumerate((forward, backward)):
            block = returned[slot_of(zh, 2 * b + d)]
            for c in range(4):
                ref[c, b] = block[2 * c : 2 * c + 2]


def shards(sections, launch_mode):
    sections = sections.reshape(4, 16, 4, 2, 8, M)
    send = pl.pallas_call(
        gather_kernel,
        out_shape=jax.ShapeDtypeStruct((16, 4, 4, 2, 8, M), F32),
        in_specs=[HBM_SPEC],
        out_specs=VMEM_SPEC,
        scratch_shapes=[pltpu.SemaphoreType.DMA((4, 4))],
        compiler_params=PARAMS,
        name="gather",
    )(sections)
    recv = lax.all_to_all(send.reshape(64, 4, 2, 8, M), ("y", "core", "zl"), 0, 0)
    recv = recv.reshape(16, 4, 4, 2, 8, M)
    total, keep = pl.pallas_call(
        tree_kernel,
        out_shape=(
            jax.ShapeDtypeStruct((2, M, M), F32),
            jax.ShapeDtypeStruct((7, 2, M, M), F32),
        ),
        in_specs=[VMEM_SPEC],
        out_specs=(VMEM_SPEC, VMEM_SPEC),
        compiler_params=PARAMS,
        name="tree",
    )(recv)
    turn = [(x, x ^ 1) for x in range(4)]
    flip = [(z, 7 - z) for z in range(8)]
    both = [(8 * x + z, 8 * (x ^ 1) + 7 - z) for x in range(4) for z in range(8)]
    near = lax.ppermute(total, ("zh", "zl"), flip)
    beside = lax.ppermute(total, "x", turn)
    across = lax.ppermute(total, ("x", "zh", "zl"), both)
    middle = pl.pallas_call(
        middle_kernel,
        out_shape=jax.ShapeDtypeStruct((8, M), F32),
        in_specs=[SMEM_SPEC] + [VMEM_SPEC] * 4,
        out_specs=VMEM_SPEC,
        scratch_shapes=[pltpu.VMEM((4, 2, M, M), F32)],
        compiler_params=PARAMS,
        name="middle",
    )(launch_mode, total, near, beside, across)
    middle = lax.ppermute(middle, "x", [(x, x ^ 2) for x in range(4)])
    fields = pl.pallas_call(
        fields_kernel,
        out_shape=jax.ShapeDtypeStruct((4, 8, M), F32),
        in_specs=[SMEM_SPEC] + [VMEM_SPEC] * 7,
        out_specs=VMEM_SPEC,
        scratch_shapes=[pltpu.VMEM((4, 2, M, M), F32)],
        compiler_params=PARAMS,
        name="fields",
    )(launch_mode, total, near, beside, across, middle, recv, keep)
    returned = lax.all_to_all(fields, "zl", 0, 0)
    return pl.pallas_call(
        output_kernel,
        out_shape=(
            jax.ShapeDtypeStruct((4, 2, 2, M), F32),
            jax.ShapeDtypeStruct((4, 2, 2, M), F32),
        ),
        in_specs=[VMEM_SPEC],
        out_specs=(VMEM_SPEC, VMEM_SPEC),
        compiler_params=PARAMS,
        name="outputs",
    )(returned)


def solution(mesh):
    fine = Mesh(mesh.devices.reshape(8, 2, 4, 2, 4), ("y", "core", "x", "zh", "zl"))
    return jax.shard_map(
        shards,
        mesh=fine,
        in_specs=(P(("x", "zh", "zl"), None, None, None, ("y", "core"), None), P(("y", "core"))),
        out_specs=(
            P(("x", "zh", "zl"), ("y", "core"), None, None),
            P(("x", "zh", "zl"), ("y", "core"), None, None),
        ),
        check_vma=False,
    )
```

```python
import functools
import math

import jax
import jax.numpy as jnp
from jax import lax
from jax.experimental import pallas as pl
from jax.experimental.pallas import tpu as pltpu
from jax.sharding import Mesh, PartitionSpec as P

M = 128
F32 = jnp.float32
BF16 = jnp.bfloat16
VMEM_SPEC = pl.BlockSpec(memory_space=pltpu.VMEM)
SMEM_SPEC = pl.BlockSpec(memory_space=pltpu.SMEM)
HBM_SPEC = pl.BlockSpec(memory_space=pltpu.HBM)
PARAMS = pltpu.CompilerParams(vmem_limit_bytes=24 * 1024 * 1024)


def slot_of(zh, zl):
    return jnp.where(zh == 0, zl, 3 - zl)


def place():
    x, zh, zl = lax.axis_index("x"), lax.axis_index("zh"), lax.axis_index("zl")
    slot = slot_of(zh, zl)
    direction = lax.rem(slot, 2)
    spot = 2 * x + zh
    spot = jnp.where(direction == 0, spot, 7 - spot)
    return slot // 2, direction, lax.rem(spot, 4), spot // 4


def gather_kernel(sections, out, stage, read_sem, sem):
    zh = lax.axis_index("zh")
    reads = []
    for c in range(4):
        for part in range(4):
            rows = pl.ds(4 * part, 4)
            read = pltpu.make_async_copy(
                sections.at[c, rows], stage.at[c, rows], read_sem.at[c, part]
            )
            read.start()
            reads.append(read)
    copies = []
    for c in range(4):
        for read in reads[4 * c : 4 * c + 4]:
            read.wait()
        for zl in range(4):
            copy = pltpu.make_async_copy(
                stage.at[c, :, slot_of(zh, zl)], out.at[:, zl, c], sem.at[zl, c]
            )
            copy.start()
            copies.append(copy)
    for copy in copies:
        copy.wait()


def split(value):
    high = value.astype(BF16)
    return high, (value - high.astype(F32)).astype(BF16)


def as_left(mat):
    high, low = split(jnp.concatenate(mat, axis=1))
    return jnp.concatenate([high, low], axis=0), high


def as_right(mat):
    real, imag = mat
    real_high, real_low = split(real)
    imag_high, imag_low = split(imag)
    high = jnp.concatenate(
        [
            jnp.concatenate([real_high, imag_high], axis=1),
            jnp.concatenate([-imag_high, real_high], axis=1),
        ],
        axis=0,
    )
    low = jnp.concatenate(
        [
            jnp.concatenate([real_low, imag_low], axis=1),
            jnp.concatenate([-imag_low, real_low], axis=1),
        ],
        axis=0,
    )
    return high, low


def product(outer_mat, inner_mat):
    both, high = as_left(outer_mat)
    right_high, right_low = as_right(inner_mat)
    wide = jnp.dot(both, right_high, preferred_element_type=F32)
    more = jnp.dot(high, right_low, preferred_element_type=F32)
    total = wide[:M] + (wide[M:] + more)
    return total[:, :M], total[:, M:]


def section_of(recv, order, step):
    index = jnp.where(order == 0, step, 15 - step)
    zl, c = index // 4, lax.rem(index, 4)
    return tuple(recv[:, zl, c, part].reshape(M, M) for part in range(2))


def tree_kernel(recv, total, keep):
    _, direction, _, _ = place()
    level = [section_of(recv, direction, step) for step in range(16)]
    kept = 0
    while len(level) > 1:
        level = [product(level[2 * k + 1], level[2 * k]) for k in range(len(level) // 2)]
        if len(level) > 1:
            for k in range(0, len(level), 2):
                for part in range(2):
                    keep[kept, part] = level[k][part]
                kept += 1
    for part in range(2):
        total[part] = level[0][part]


def matvec(mat, vec, eye):
    mat_real, mat_imag = mat
    real, imag = vec
    out_real = jnp.sum(mat_real * real - mat_imag * imag, axis=1, keepdims=True)
    out_imag = jnp.sum(mat_real * imag + mat_imag * real, axis=1, keepdims=True)
    return (
        jnp.sum(jnp.where(eye, out_real, 0.0), axis=0, keepdims=True),
        jnp.sum(jnp.where(eye, out_imag, 0.0), axis=0, keepdims=True),
    )


def diagonal():
    return lax.broadcasted_iota(jnp.int32, (M, M), 0) == lax.broadcasted_iota(jnp.int32, (M, M), 1)


def launch_vector(mode, b):
    lane = lax.broadcasted_iota(jnp.int32, (1, M), 1)
    onehot = jnp.where(lane == mode[b], jnp.float32(math.sqrt(M)), 0.0)
    return onehot, jnp.zeros_like(onehot)


def pair_kernel(own, near, pair):
    _, _, spot, _ = place()
    odd = lax.rem(spot, 2) == 1
    first = tuple(jnp.where(odd, near[part], own[part]) for part in range(2))
    second = tuple(jnp.where(odd, own[part], near[part]) for part in range(2))
    result = product(second, first)
    for part in range(2):
        for s in range(4):
            pair[s, part] = result[part]


def fields_kernel(mode, own, near, mats, recv, keep, out):
    b, direction, spot, upper = place()
    column = 2 * upper + spot // 2
    eye = diagonal()

    def enter(step, vec):
        which = jnp.where(direction == 0, step, 3 - step)
        return matvec((mats[which, 0], mats[which, 1]), vec, eye)

    vec = lax.fori_loop(0, column, enter, launch_vector(mode, b))

    def step_in(step, vec):
        return matvec((near[0], near[1]), vec, eye)

    states = [None] * 17
    states[0] = lax.fori_loop(0, lax.rem(spot, 2), step_in, vec)

    def kept(k):
        return keep[k, 0], keep[k, 1]

    states[16] = matvec((own[0], own[1]), states[0], eye)
    states[8] = matvec(kept(6), states[0], eye)
    for k in range(2):
        states[8 * k + 4] = matvec(kept(4 + k), states[8 * k], eye)
    for k in range(4):
        states[4 * k + 2] = matvec(kept(k), states[4 * k], eye)
    for k in range(8):
        states[2 * k + 1] = matvec(section_of(recv, direction, 2 * k), states[2 * k], eye)
    for index in range(16):
        for part in range(2):
            out[index // 4, 2 * (index % 4) + part : 2 * (index % 4) + part + 1] = jnp.where(
                direction == 0, states[index + 1][part], states[15 - index][part]
            )


def output_kernel(returned, forward, backward):
    zh = lax.axis_index("zh")
    for b in range(2):
        for d, ref in enumerate((forward, backward)):
            block = returned[slot_of(zh, 2 * b + d)]
            for c in range(4):
                ref[c, b] = block[2 * c : 2 * c + 2]


def shards(sections, launch_mode):
    sections = sections.reshape(4, 16, 4, 2, 8, M)
    send = pl.pallas_call(
        gather_kernel,
        out_shape=jax.ShapeDtypeStruct((16, 4, 4, 2, 8, M), F32),
        in_specs=[HBM_SPEC],
        out_specs=VMEM_SPEC,
        scratch_shapes=[
            pltpu.VMEM((4, 16, 4, 2, 8, M), F32),
            pltpu.SemaphoreType.DMA((4, 4)),
            pltpu.SemaphoreType.DMA((4, 4)),
        ],
        compiler_params=pltpu.CompilerParams(vmem_limit_bytes=60 * 1024 * 1024),
        name="gather",
    )(sections)
    recv = lax.all_to_all(send.reshape(64, 4, 2, 8, M), ("y", "core", "zl"), 0, 0)
    recv = recv.reshape(16, 4, 4, 2, 8, M)
    total, keep = pl.pallas_call(
        tree_kernel,
        out_shape=(
            jax.ShapeDtypeStruct((2, M, M), F32),
            jax.ShapeDtypeStruct((7, 2, M, M), F32),
        ),
        in_specs=[VMEM_SPEC],
        out_specs=(VMEM_SPEC, VMEM_SPEC),
        compiler_params=PARAMS,
        name="tree",
    )(recv)
    near = lax.ppermute(total, ("zh", "zl"), [(z, 7 - z) for z in range(8)])
    pair = pl.pallas_call(
        pair_kernel,
        out_shape=jax.ShapeDtypeStruct((4, 2, M, M), F32),
        in_specs=[VMEM_SPEC] * 2,
        out_specs=VMEM_SPEC,
        compiler_params=PARAMS,
        name="pair",
    )(total, near)
    mats = lax.all_to_all(pair, "x", 0, 0)
    fields = pl.pallas_call(
        fields_kernel,
        out_shape=jax.ShapeDtypeStruct((4, 8, M), F32),
        in_specs=[SMEM_SPEC] + [VMEM_SPEC] * 5,
        out_specs=VMEM_SPEC,
        compiler_params=PARAMS,
        name="fields",
    )(launch_mode, total, near, mats, recv, keep)
    returned = lax.all_to_all(fields, "zl", 0, 0)
    return pl.pallas_call(
        output_kernel,
        out_shape=(
            jax.ShapeDtypeStruct((4, 2, 2, M), F32),
            jax.ShapeDtypeStruct((4, 2, 2, M), F32),
        ),
        in_specs=[VMEM_SPEC],
        out_specs=(VMEM_SPEC, VMEM_SPEC),
        compiler_params=PARAMS,
        name="outputs",
    )(returned)


def solution(mesh):
    fine = Mesh(mesh.devices.reshape(8, 2, 4, 2, 4), ("y", "core", "x", "zh", "zl"))
    return jax.shard_map(
        shards,
        mesh=fine,
        in_specs=(P(("x", "zh", "zl"), None, None, None, ("y", "core"), None), P(("y", "core"))),
        out_specs=(
            P(("x", "zh", "zl"), ("y", "core"), None, None),
            P(("x", "zh", "zl"), ("y", "core"), None, None),
        ),
        check_vma=False,
    )
```

```python
import math

import jax
import jax.numpy as jnp
from jax import lax
from jax.experimental import pallas as pl
from jax.experimental.pallas import tpu as pltpu
from jax.sharding import Mesh, PartitionSpec as P

M = 128
F32 = jnp.float32
BF16 = jnp.bfloat16
VMEM_SPEC = pl.BlockSpec(memory_space=pltpu.VMEM)
SMEM_SPEC = pl.BlockSpec(memory_space=pltpu.SMEM)
HBM_SPEC = pl.BlockSpec(memory_space=pltpu.HBM)
PARAMS = pltpu.CompilerParams(vmem_limit_bytes=24 * 1024 * 1024)


def slot_of(zh, zl):
    return jnp.where(zh == 0, zl, 3 - zl)


def place():
    x, zh, zl = lax.axis_index("x"), lax.axis_index("zh"), lax.axis_index("zl")
    slot = slot_of(zh, zl)
    direction = lax.rem(slot, 2)
    spot = 2 * x + zh
    spot = jnp.where(direction == 0, spot, 7 - spot)
    return slot // 2, direction, lax.rem(spot, 4), spot // 4


def gather_kernel(sections, out, sem):
    zh = lax.axis_index("zh")
    copies = []
    for zl in range(4):
        slot = slot_of(zh, zl)
        for c in range(4):
            copy = pltpu.make_async_copy(sections.at[c, :, slot], out.at[:, zl, c], sem.at[zl, c])
            copy.start()
            copies.append(copy)
    for copy in copies:
        copy.wait()


def split(value):
    high = value.astype(BF16)
    return high, (value - high.astype(F32)).astype(BF16)


def as_left(mat):
    high, low = split(jnp.concatenate(mat, axis=1))
    return jnp.concatenate([high, low], axis=0), high


def as_right(mat):
    real, imag = mat
    real_high, real_low = split(real)
    imag_high, imag_low = split(imag)
    high = jnp.concatenate(
        [
            jnp.concatenate([real_high, imag_high], axis=1),
            jnp.concatenate([-imag_high, real_high], axis=1),
        ],
        axis=0,
    )
    low = jnp.concatenate(
        [
            jnp.concatenate([real_low, imag_low], axis=1),
            jnp.concatenate([-imag_low, real_low], axis=1),
        ],
        axis=0,
    )
    return high, low


def product(outer_mat, inner_mat):
    both, high = as_left(outer_mat)
    right_high, right_low = as_right(inner_mat)
    wide = jnp.dot(both, right_high, preferred_element_type=F32)
    more = jnp.dot(high, right_low, preferred_element_type=F32)
    total = wide[:M] + (wide[M:] + more)
    return total[:, :M], total[:, M:]


def section_of(recv, order, step):
    index = jnp.where(order == 0, step, 15 - step)
    zl, c = index // 4, lax.rem(index, 4)
    return tuple(recv[:, zl, c, part].reshape(M, M) for part in range(2))


def tree_kernel(recv, total, keep):
    _, direction, _, _ = place()
    level = [section_of(recv, direction, step) for step in range(16)]
    kept = 0
    while len(level) > 1:
        level = [product(level[2 * k + 1], level[2 * k]) for k in range(len(level) // 2)]
        if len(level) > 1:
            for k in range(0, len(level), 2):
                for part in range(2):
                    keep[kept, part] = level[k][part]
                kept += 1
    for part in range(2):
        total[part] = level[0][part]


def matvec(mat, vec, eye):
    mat_real, mat_imag = mat
    real, imag = vec
    out_real = jnp.sum(mat_real * real - mat_imag * imag, axis=1, keepdims=True)
    out_imag = jnp.sum(mat_real * imag + mat_imag * real, axis=1, keepdims=True)
    return (
        jnp.sum(jnp.where(eye, out_real, 0.0), axis=0, keepdims=True),
        jnp.sum(jnp.where(eye, out_imag, 0.0), axis=0, keepdims=True),
    )


def diagonal():
    return lax.broadcasted_iota(jnp.int32, (M, M), 0) == lax.broadcasted_iota(jnp.int32, (M, M), 1)


def launch_vector(mode, b):
    lane = lax.broadcasted_iota(jnp.int32, (1, M), 1)
    onehot = jnp.where(lane == mode[b], jnp.float32(math.sqrt(M)), 0.0)
    return onehot, jnp.zeros_like(onehot)


def prefix_kernel(recv, keep, total, turned):
    _, direction, _, _ = place()

    def kept(k):
        return keep[k, 0], keep[k, 1]

    def section(step):
        return section_of(recv, direction, step)

    prefix = {1: section(0), 2: kept(0), 4: kept(4), 8: kept(6), 16: (total[0], total[1])}
    prefix[6] = product(kept(1), prefix[4])
    prefix[10] = product(kept(2), prefix[8])
    prefix[12] = product(kept(5), prefix[8])
    prefix[14] = product(kept(3), prefix[12])
    for step in range(2, 16, 2):
        prefix[step + 1] = product(section(step), prefix[step])
    for step in range(1, 17):
        for part in range(2):
            turned[step - 1, part] = prefix[step][part].T


def pair_kernel(own, near, turned, pair):
    del turned
    _, _, spot, _ = place()
    odd = lax.rem(spot, 2) == 1
    first = tuple(jnp.where(odd, near[part], own[part]) for part in range(2))
    second = tuple(jnp.where(odd, own[part], near[part]) for part in range(2))
    result = product(second, first)
    for part in range(2):
        for s in range(4):
            pair[s, part] = result[part]


def fields_kernel(mode, near, mats, turned, out):
    b, direction, spot, upper = place()
    column = 2 * upper + spot // 2
    eye = diagonal()

    def enter(step, vec):
        which = jnp.where(direction == 0, step, 3 - step)
        return matvec((mats[which, 0], mats[which, 1]), vec, eye)

    vec = lax.fori_loop(0, column, enter, launch_vector(mode, b))

    def step_in(step, vec):
        return matvec((near[0], near[1]), vec, eye)

    entering = lax.fori_loop(0, lax.rem(spot, 2), step_in, vec)
    real, imag = (
        jnp.sum(jnp.where(eye, entering[part], 0.0), axis=1, keepdims=True) for part in range(2)
    )
    states = [entering]
    for step in range(16):
        mat_real, mat_imag = turned[step, 0], turned[step, 1]
        states.append(
            (
                jnp.sum(mat_real * real - mat_imag * imag, axis=0, keepdims=True),
                jnp.sum(mat_real * imag + mat_imag * real, axis=0, keepdims=True),
            )
        )
    for index in range(16):
        for part in range(2):
            out[index // 4, 2 * (index % 4) + part : 2 * (index % 4) + part + 1] = jnp.where(
                direction == 0, states[index + 1][part], states[15 - index][part]
            )


def output_kernel(returned, forward, backward):
    zh = lax.axis_index("zh")
    for b in range(2):
        for d, ref in enumerate((forward, backward)):
            block = returned[slot_of(zh, 2 * b + d)]
            for c in range(4):
                ref[c, b] = block[2 * c : 2 * c + 2]


def shards(sections, launch_mode):
    sections = sections.reshape(4, 16, 4, 2, 8, M)
    send = pl.pallas_call(
        gather_kernel,
        out_shape=jax.ShapeDtypeStruct((16, 4, 4, 2, 8, M), F32),
        in_specs=[HBM_SPEC],
        out_specs=VMEM_SPEC,
        scratch_shapes=[pltpu.SemaphoreType.DMA((4, 4))],
        compiler_params=PARAMS,
        name="gather",
    )(sections)
    recv = lax.all_to_all(send.reshape(64, 4, 2, 8, M), ("y", "core", "zl"), 0, 0)
    recv = recv.reshape(16, 4, 4, 2, 8, M)
    total, keep = pl.pallas_call(
        tree_kernel,
        out_shape=(
            jax.ShapeDtypeStruct((2, M, M), F32),
            jax.ShapeDtypeStruct((7, 2, M, M), F32),
        ),
        in_specs=[VMEM_SPEC],
        out_specs=(VMEM_SPEC, VMEM_SPEC),
        compiler_params=PARAMS,
        name="tree",
    )(recv)
    near = lax.ppermute(total, ("zh", "zl"), [(z, 7 - z) for z in range(8)])
    turned = pl.pallas_call(
        prefix_kernel,
        out_shape=jax.ShapeDtypeStruct((16, 2, M, M), F32),
        in_specs=[VMEM_SPEC] * 3,
        out_specs=VMEM_SPEC,
        compiler_params=PARAMS,
        cost_estimate=pl.CostEstimate(
            flops=11 * 6 * 8 * M * M * M, bytes_accessed=6 * 1024 * 1024, transcendentals=0
        ),
        name="prefix",
    )(recv, keep, total)
    pair = pl.pallas_call(
        pair_kernel,
        out_shape=jax.ShapeDtypeStruct((4, 2, M, M), F32),
        in_specs=[VMEM_SPEC] * 3,
        out_specs=VMEM_SPEC,
        compiler_params=PARAMS,
        name="pair",
    )(total, near, turned)
    mats = lax.all_to_all(pair, "x", 0, 0)
    fields = pl.pallas_call(
        fields_kernel,
        out_shape=jax.ShapeDtypeStruct((4, 8, M), F32),
        in_specs=[SMEM_SPEC] + [VMEM_SPEC] * 3,
        out_specs=VMEM_SPEC,
        compiler_params=PARAMS,
        name="fields",
    )(launch_mode, near, mats, turned)
    returned = lax.all_to_all(fields, "zl", 0, 0)
    return pl.pallas_call(
        output_kernel,
        out_shape=(
            jax.ShapeDtypeStruct((4, 2, 2, M), F32),
            jax.ShapeDtypeStruct((4, 2, 2, M), F32),
        ),
        in_specs=[VMEM_SPEC],
        out_specs=(VMEM_SPEC, VMEM_SPEC),
        compiler_params=PARAMS,
        name="outputs",
    )(returned)


def solution(mesh):
    fine = Mesh(mesh.devices.reshape(8, 2, 4, 2, 4), ("y", "core", "x", "zh", "zl"))
    return jax.shard_map(
        shards,
        mesh=fine,
        in_specs=(P(("x", "zh", "zl"), None, None, None, ("y", "core"), None), P(("y", "core"))),
        out_specs=(
            P(("x", "zh", "zl"), ("y", "core"), None, None),
            P(("x", "zh", "zl"), ("y", "core"), None, None),
        ),
        check_vma=False,
    )
```

```python
import math

import jax
import jax.numpy as jnp
from jax import lax
from jax.experimental import pallas as pl
from jax.experimental.pallas import tpu as pltpu
from jax.sharding import Mesh, PartitionSpec as P

M = 128
F32 = jnp.float32
BF16 = jnp.bfloat16
VMEM_SPEC = pl.BlockSpec(memory_space=pltpu.VMEM)
SMEM_SPEC = pl.BlockSpec(memory_space=pltpu.SMEM)
HBM_SPEC = pl.BlockSpec(memory_space=pltpu.HBM)
PARAMS = pltpu.CompilerParams(vmem_limit_bytes=24 * 1024 * 1024)


def slot_of(zh, zl):
    return zl ^ (2 * zh)


def place():
    x, zh, zl = lax.axis_index("x"), lax.axis_index("zh"), lax.axis_index("zl")
    slot = slot_of(zh, zl)
    direction = lax.rem(slot, 2)
    spot = 2 * x + zh
    spot = jnp.where(direction == 0, spot, 7 - spot)
    return slot // 2, direction, lax.rem(spot, 4), spot // 4


def gather_kernel(sections, out, sem):
    zh = lax.axis_index("zh")
    copies = []
    for zl in range(4):
        slot = slot_of(zh, zl)
        for c in range(4):
            copy = pltpu.make_async_copy(sections.at[c, :, slot], out.at[:, zl, c], sem.at[zl, c])
            copy.start()
            copies.append(copy)
    for copy in copies:
        copy.wait()


def split(value):
    high = value.astype(BF16)
    return high, (value - high.astype(F32)).astype(BF16)


def as_left(mat):
    high, low = split(jnp.concatenate(mat, axis=1))
    return jnp.concatenate([high, low], axis=0), high


def as_right(mat):
    real, imag = mat
    real_high, real_low = split(real)
    imag_high, imag_low = split(imag)
    high = jnp.concatenate(
        [
            jnp.concatenate([real_high, imag_high], axis=1),
            jnp.concatenate([-imag_high, real_high], axis=1),
        ],
        axis=0,
    )
    low = jnp.concatenate(
        [
            jnp.concatenate([real_low, imag_low], axis=1),
            jnp.concatenate([-imag_low, real_low], axis=1),
        ],
        axis=0,
    )
    return high, low


def product(outer_mat, inner_mat):
    both, high = as_left(outer_mat)
    right_high, right_low = as_right(inner_mat)
    wide = jnp.dot(both, right_high, preferred_element_type=F32)
    more = jnp.dot(high, right_low, preferred_element_type=F32)
    total = wide[:M] + (wide[M:] + more)
    return total[:, :M], total[:, M:]


def section_of(recv, order, step):
    index = jnp.where(order == 0, step, 15 - step)
    zl, c = index // 4, lax.rem(index, 4)
    return tuple(recv[:, zl, c, part].reshape(M, M) for part in range(2))


def tree_kernel(recv, total, keep):
    _, direction, _, _ = place()
    level = [section_of(recv, direction, step) for step in range(16)]
    kept = 0
    while len(level) > 1:
        level = [product(level[2 * k + 1], level[2 * k]) for k in range(len(level) // 2)]
        if len(level) > 1:
            for k in range(0, len(level), 2):
                for part in range(2):
                    keep[kept, part] = level[k][part]
                kept += 1
    for part in range(2):
        total[part] = level[0][part]


def matvec(mat, vec, eye):
    mat_real, mat_imag = mat
    real, imag = vec
    out_real = jnp.sum(mat_real * real - mat_imag * imag, axis=1, keepdims=True)
    out_imag = jnp.sum(mat_real * imag + mat_imag * real, axis=1, keepdims=True)
    return (
        jnp.sum(jnp.where(eye, out_real, 0.0), axis=0, keepdims=True),
        jnp.sum(jnp.where(eye, out_imag, 0.0), axis=0, keepdims=True),
    )


def diagonal():
    return lax.broadcasted_iota(jnp.int32, (M, M), 0) == lax.broadcasted_iota(jnp.int32, (M, M), 1)


def launch_vector(mode, b):
    lane = lax.broadcasted_iota(jnp.int32, (1, M), 1)
    onehot = jnp.where(lane == mode[b], jnp.float32(math.sqrt(M)), 0.0)
    return onehot, jnp.zeros_like(onehot)


def prefix_kernel(recv, keep, total, turned):
    _, direction, _, _ = place()

    def kept(k):
        return keep[k, 0], keep[k, 1]

    def section(step):
        return section_of(recv, direction, step)

    prefix = {1: section(0), 2: kept(0), 4: kept(4), 8: kept(6), 16: (total[0], total[1])}
    prefix[6] = product(kept(1), prefix[4])
    prefix[10] = product(kept(2), prefix[8])
    prefix[12] = product(kept(5), prefix[8])
    prefix[14] = product(kept(3), prefix[12])
    for step in range(2, 16, 2):
        prefix[step + 1] = product(section(step), prefix[step])
    eye = jnp.where(diagonal(), 1.0, 0.0)
    prefix[0] = (eye, jnp.zeros_like(eye))
    flat = {step: tuple(part.T for part in prefix[step]) for step in range(17)}
    for index in range(16):
        for part in range(2):
            turned[index, part] = jnp.where(
                direction == 0, flat[index + 1][part], flat[15 - index][part]
            )


def pair_kernel(own, near, turned, pair):
    del turned
    _, _, spot, _ = place()
    odd = lax.rem(spot, 2) == 1
    first = tuple(jnp.where(odd, near[part], own[part]) for part in range(2))
    second = tuple(jnp.where(odd, own[part], near[part]) for part in range(2))
    result = product(second, first)
    for part in range(2):
        for s in range(4):
            pair[s, part] = result[part]


def fields_kernel(mode, near, mats, turned, out):
    b, direction, spot, upper = place()
    column = 2 * upper + spot // 2
    eye = diagonal()

    def enter(step, vec):
        which = jnp.where(direction == 0, step, 3 - step)
        return matvec((mats[which, 0], mats[which, 1]), vec, eye)

    vec = lax.fori_loop(0, column, enter, launch_vector(mode, b))

    def step_in(step, vec):
        return matvec((near[0], near[1]), vec, eye)

    entering = lax.fori_loop(0, lax.rem(spot, 2), step_in, vec)
    real, imag = (
        jnp.sum(jnp.where(eye, entering[part], 0.0), axis=1, keepdims=True) for part in range(2)
    )
    for index in range(16):
        mat_real, mat_imag = turned[index, 0], turned[index, 1]
        row = 2 * (index % 4)
        out[index // 4, row : row + 1] = jnp.sum(
            mat_real * real - mat_imag * imag, axis=0, keepdims=True
        )
        out[index // 4, row + 1 : row + 2] = jnp.sum(
            mat_real * imag + mat_imag * real, axis=0, keepdims=True
        )


def output_kernel(returned, forward, backward):
    zh = lax.axis_index("zh")
    for b in range(2):
        for d, ref in enumerate((forward, backward)):
            block = returned[slot_of(zh, 2 * b + d)]
            for c in range(4):
                ref[c, b] = block[2 * c : 2 * c + 2]


def shards(sections, launch_mode):
    sections = sections.reshape(4, 16, 4, 2, 8, M)
    send = pl.pallas_call(
        gather_kernel,
        out_shape=jax.ShapeDtypeStruct((16, 4, 4, 2, 8, M), F32),
        in_specs=[HBM_SPEC],
        out_specs=VMEM_SPEC,
        scratch_shapes=[pltpu.SemaphoreType.DMA((4, 4))],
        compiler_params=PARAMS,
        name="gather",
    )(sections)
    recv = lax.all_to_all(send.reshape(64, 4, 2, 8, M), ("y", "core", "zl"), 0, 0)
    recv = recv.reshape(16, 4, 4, 2, 8, M)
    total, keep = pl.pallas_call(
        tree_kernel,
        out_shape=(
            jax.ShapeDtypeStruct((2, M, M), F32),
            jax.ShapeDtypeStruct((7, 2, M, M), F32),
        ),
        in_specs=[VMEM_SPEC],
        out_specs=(VMEM_SPEC, VMEM_SPEC),
        compiler_params=PARAMS,
        name="tree",
    )(recv)
    near = lax.ppermute(total, ("zh", "zl"), [(z, z ^ 6) for z in range(8)])
    turned = pl.pallas_call(
        prefix_kernel,
        out_shape=jax.ShapeDtypeStruct((16, 2, M, M), F32),
        in_specs=[VMEM_SPEC] * 3,
        out_specs=VMEM_SPEC,
        compiler_params=PARAMS,
        cost_estimate=pl.CostEstimate(
            flops=11 * 6 * 8 * M * M * M, bytes_accessed=6 * 1024 * 1024, transcendentals=0
        ),
        name="prefix",
    )(recv, keep, total)
    pair = pl.pallas_call(
        pair_kernel,
        out_shape=jax.ShapeDtypeStruct((4, 2, M, M), F32),
        in_specs=[VMEM_SPEC] * 3,
        out_specs=VMEM_SPEC,
        compiler_params=PARAMS,
        name="pair",
    )(total, near, turned)
    mats = lax.all_to_all(pair, "x", 0, 0)
    fields = pl.pallas_call(
        fields_kernel,
        out_shape=jax.ShapeDtypeStruct((4, 8, M), F32),
        in_specs=[SMEM_SPEC] + [VMEM_SPEC] * 3,
        out_specs=VMEM_SPEC,
        compiler_params=PARAMS,
        name="fields",
    )(launch_mode, near, mats, turned)
    returned = lax.all_to_all(fields, "zl", 0, 0)
    return pl.pallas_call(
        output_kernel,
        out_shape=(
            jax.ShapeDtypeStruct((4, 2, 2, M), F32),
            jax.ShapeDtypeStruct((4, 2, 2, M), F32),
        ),
        in_specs=[VMEM_SPEC],
        out_specs=(VMEM_SPEC, VMEM_SPEC),
        compiler_params=PARAMS,
        name="outputs",
    )(returned)


def solution(mesh):
    fine = Mesh(mesh.devices.reshape(8, 2, 4, 2, 4), ("y", "core", "x", "zh", "zl"))
    return jax.shard_map(
        shards,
        mesh=fine,
        in_specs=(P(("x", "zh", "zl"), None, None, None, ("y", "core"), None), P(("y", "core"))),
        out_specs=(
            P(("x", "zh", "zl"), ("y", "core"), None, None),
            P(("x", "zh", "zl"), ("y", "core"), None, None),
        ),
        check_vma=False,
    )
```

```python
import math

import jax
import jax.numpy as jnp
from jax import lax
from jax.experimental import pallas as pl
from jax.experimental.pallas import tpu as pltpu
from jax.sharding import Mesh, PartitionSpec as P

M = 128
F32 = jnp.float32
BF16 = jnp.bfloat16
VMEM_SPEC = pl.BlockSpec(memory_space=pltpu.VMEM)
SMEM_SPEC = pl.BlockSpec(memory_space=pltpu.SMEM)
HBM_SPEC = pl.BlockSpec(memory_space=pltpu.HBM)
PARAMS = pltpu.CompilerParams(vmem_limit_bytes=24 * 1024 * 1024)


def slot_of(zh, zl):
    return zl ^ (3 - 3 * zh)


def place():
    x, zh, zl = lax.axis_index("x"), lax.axis_index("zh"), lax.axis_index("zl")
    slot = slot_of(zh, zl)
    direction = lax.rem(slot, 2)
    spot = 2 * x + zh
    spot = jnp.where(direction == 0, spot, 7 - spot)
    return slot // 2, direction, lax.rem(spot, 4), spot // 4


def gather_kernel(sections, out, sem):
    zh = lax.axis_index("zh")

    @pl.when(zh == 1)
    def _():
        copies = [
            pltpu.make_async_copy(sections.at[c], out.at[:, :, c], sem.at[0, c]) for c in range(4)
        ]
        for copy in copies:
            copy.start()
        for copy in copies:
            copy.wait()

    @pl.when(zh == 0)
    def _():
        copies = [
            pltpu.make_async_copy(sections.at[c, :, 3 - zl], out.at[:, zl, c], sem.at[zl, c])
            for zl in range(4)
            for c in range(4)
        ]
        for copy in copies:
            copy.start()
        for copy in copies:
            copy.wait()


def split(value):
    high = value.astype(BF16)
    return high, (value - high.astype(F32)).astype(BF16)


def as_left(mat):
    high, low = split(jnp.concatenate(mat, axis=1))
    return jnp.concatenate([high, low], axis=0), high


def as_right(mat):
    real, imag = mat
    real_high, real_low = split(real)
    imag_high, imag_low = split(imag)
    high = jnp.concatenate(
        [
            jnp.concatenate([real_high, imag_high], axis=1),
            jnp.concatenate([-imag_high, real_high], axis=1),
        ],
        axis=0,
    )
    low = jnp.concatenate(
        [
            jnp.concatenate([real_low, imag_low], axis=1),
            jnp.concatenate([-imag_low, real_low], axis=1),
        ],
        axis=0,
    )
    return high, low


def product(outer_mat, inner_mat):
    both, high = as_left(outer_mat)
    right_high, right_low = as_right(inner_mat)
    wide = jnp.dot(both, right_high, preferred_element_type=F32)
    more = jnp.dot(high, right_low, preferred_element_type=F32)
    total = wide[:M] + (wide[M:] + more)
    return total[:, :M], total[:, M:]


def section_of(recv, order, step):
    index = jnp.where(order == 0, step, 15 - step)
    zl, c = index // 4, lax.rem(index, 4)
    return tuple(recv[:, zl, c, part].reshape(M, M) for part in range(2))


def tree_kernel(recv, total, keep):
    _, direction, _, _ = place()
    level = [section_of(recv, direction, step) for step in range(16)]
    kept = 0
    while len(level) > 1:
        level = [product(level[2 * k + 1], level[2 * k]) for k in range(len(level) // 2)]
        if len(level) > 1:
            for k in range(0, len(level), 2):
                for part in range(2):
                    keep[kept, part] = level[k][part]
                kept += 1
    for part in range(2):
        total[part] = level[0][part]


def matvec(mat, vec, eye):
    mat_real, mat_imag = mat
    real, imag = vec
    out_real = jnp.sum(mat_real * real - mat_imag * imag, axis=1, keepdims=True)
    out_imag = jnp.sum(mat_real * imag + mat_imag * real, axis=1, keepdims=True)
    return (
        jnp.sum(jnp.where(eye, out_real, 0.0), axis=0, keepdims=True),
        jnp.sum(jnp.where(eye, out_imag, 0.0), axis=0, keepdims=True),
    )


def diagonal():
    return lax.broadcasted_iota(jnp.int32, (M, M), 0) == lax.broadcasted_iota(jnp.int32, (M, M), 1)


def launch_vector(mode, b):
    lane = lax.broadcasted_iota(jnp.int32, (1, M), 1)
    onehot = jnp.where(lane == mode[b], jnp.float32(math.sqrt(M)), 0.0)
    return onehot, jnp.zeros_like(onehot)


def prefix_kernel(recv, keep, total, turned):
    _, direction, _, _ = place()

    def kept(k):
        return keep[k, 0], keep[k, 1]

    def section(step):
        return section_of(recv, direction, step)

    prefix = {1: section(0), 2: kept(0), 4: kept(4), 8: kept(6), 16: (total[0], total[1])}
    prefix[6] = product(kept(1), prefix[4])
    prefix[10] = product(kept(2), prefix[8])
    prefix[12] = product(kept(5), prefix[8])
    prefix[14] = product(kept(3), prefix[12])
    for step in range(2, 16, 2):
        prefix[step + 1] = product(section(step), prefix[step])
    eye = jnp.where(diagonal(), 1.0, 0.0)
    prefix[0] = (eye, jnp.zeros_like(eye))
    flat = {step: tuple(part.T for part in prefix[step]) for step in range(17)}
    for index in range(16):
        for part in range(2):
            turned[index, part] = jnp.where(
                direction == 0, flat[index + 1][part], flat[15 - index][part]
            )


def pair_kernel(own, near, turned, pair):
    del turned
    _, _, spot, _ = place()
    odd = lax.rem(spot, 2) == 1
    first = tuple(jnp.where(odd, near[part], own[part]) for part in range(2))
    second = tuple(jnp.where(odd, own[part], near[part]) for part in range(2))
    result = product(second, first)
    for part in range(2):
        for s in range(4):
            pair[s, part] = result[part]


def fields_kernel(mode, near, mats, turned, out):
    b, direction, spot, upper = place()
    column = 2 * upper + spot // 2
    eye = diagonal()

    def enter(step, vec):
        which = jnp.where(direction == 0, step, 3 - step)
        return matvec((mats[which, 0], mats[which, 1]), vec, eye)

    vec = lax.fori_loop(0, column, enter, launch_vector(mode, b))

    def step_in(step, vec):
        return matvec((near[0], near[1]), vec, eye)

    entering = lax.fori_loop(0, lax.rem(spot, 2), step_in, vec)
    real, imag = (
        jnp.sum(jnp.where(eye, entering[part], 0.0), axis=1, keepdims=True) for part in range(2)
    )
    for index in range(16):
        mat_real, mat_imag = turned[index, 0], turned[index, 1]
        row = 2 * (index % 4)
        out[index // 4, row : row + 1] = jnp.sum(
            mat_real * real - mat_imag * imag, axis=0, keepdims=True
        )
        out[index // 4, row + 1 : row + 2] = jnp.sum(
            mat_real * imag + mat_imag * real, axis=0, keepdims=True
        )


def output_kernel(returned, forward, backward):
    zh = lax.axis_index("zh")
    for b in range(2):
        for d, ref in enumerate((forward, backward)):
            block = returned[slot_of(zh, 2 * b + d)]
            for c in range(4):
                ref[c, b] = block[2 * c : 2 * c + 2]


def shards(sections, launch_mode):
    sections = sections.reshape(4, 16, 4, 2, 8, M)
    send = pl.pallas_call(
        gather_kernel,
        out_shape=jax.ShapeDtypeStruct((16, 4, 4, 2, 8, M), F32),
        in_specs=[HBM_SPEC],
        out_specs=VMEM_SPEC,
        scratch_shapes=[pltpu.SemaphoreType.DMA((4, 4))],
        compiler_params=PARAMS,
        name="gather",
    )(sections)
    recv = lax.all_to_all(send.reshape(64, 4, 2, 8, M), ("y", "core", "zl"), 0, 0)
    recv = recv.reshape(16, 4, 4, 2, 8, M)
    total, keep = pl.pallas_call(
        tree_kernel,
        out_shape=(
            jax.ShapeDtypeStruct((2, M, M), F32),
            jax.ShapeDtypeStruct((7, 2, M, M), F32),
        ),
        in_specs=[VMEM_SPEC],
        out_specs=(VMEM_SPEC, VMEM_SPEC),
        compiler_params=PARAMS,
        name="tree",
    )(recv)
    near = lax.ppermute(total, ("zh", "zl"), [(z, z ^ 7) for z in range(8)])
    turned = pl.pallas_call(
        prefix_kernel,
        out_shape=jax.ShapeDtypeStruct((16, 2, M, M), F32),
        in_specs=[VMEM_SPEC] * 3,
        out_specs=VMEM_SPEC,
        compiler_params=PARAMS,
        cost_estimate=pl.CostEstimate(
            flops=11 * 6 * 8 * M * M * M, bytes_accessed=6 * 1024 * 1024, transcendentals=0
        ),
        name="prefix",
    )(recv, keep, total)
    pair = pl.pallas_call(
        pair_kernel,
        out_shape=jax.ShapeDtypeStruct((4, 2, M, M), F32),
        in_specs=[VMEM_SPEC] * 3,
        out_specs=VMEM_SPEC,
        compiler_params=PARAMS,
        name="pair",
    )(total, near, turned)
    mats = lax.all_to_all(pair, "x", 0, 0)
    fields = pl.pallas_call(
        fields_kernel,
        out_shape=jax.ShapeDtypeStruct((4, 8, M), F32),
        in_specs=[SMEM_SPEC] + [VMEM_SPEC] * 3,
        out_specs=VMEM_SPEC,
        compiler_params=PARAMS,
        name="fields",
    )(launch_mode, near, mats, turned)
    returned = lax.all_to_all(fields, "zl", 0, 0)
    return pl.pallas_call(
        output_kernel,
        out_shape=(
            jax.ShapeDtypeStruct((4, 2, 2, M), F32),
            jax.ShapeDtypeStruct((4, 2, 2, M), F32),
        ),
        in_specs=[VMEM_SPEC],
        out_specs=(VMEM_SPEC, VMEM_SPEC),
        compiler_params=PARAMS,
        name="outputs",
    )(returned)


def solution(mesh):
    fine = Mesh(mesh.devices.reshape(8, 2, 4, 2, 4), ("y", "core", "x", "zh", "zl"))
    return jax.shard_map(
        shards,
        mesh=fine,
        in_specs=(P(("x", "zh", "zl"), None, None, None, ("y", "core"), None), P(("y", "core"))),
        out_specs=(
            P(("x", "zh", "zl"), ("y", "core"), None, None),
            P(("x", "zh", "zl"), ("y", "core"), None, None),
        ),
        check_vma=False,
    )
```

```python
import math

import jax
import jax.numpy as jnp
from jax import lax
from jax.experimental import pallas as pl
from jax.experimental.pallas import tpu as pltpu
from jax.sharding import Mesh, PartitionSpec as P

M = 128
F32 = jnp.float32
BF16 = jnp.bfloat16
VMEM_SPEC = pl.BlockSpec(memory_space=pltpu.VMEM)
SMEM_SPEC = pl.BlockSpec(memory_space=pltpu.SMEM)
HBM_SPEC = pl.BlockSpec(memory_space=pltpu.HBM)
PARAMS = pltpu.CompilerParams(vmem_limit_bytes=24 * 1024 * 1024)


def slot_of(zh, zl):
    return jnp.where(zh == 0, zl, 3 - zl)


def place():
    x, zh, zl = lax.axis_index("x"), lax.axis_index("zh"), lax.axis_index("zl")
    slot = slot_of(zh, zl)
    direction = lax.rem(slot, 2)
    spot = 2 * x + zh
    spot = jnp.where(direction == 0, spot, 7 - spot)
    return slot // 2, direction, lax.rem(spot, 4), spot // 4


def gather_kernel(sections, out, sem):
    zh = lax.axis_index("zh")
    copies = []
    for zl in range(4):
        slot = slot_of(zh, zl)
        for c in range(4):
            copy = pltpu.make_async_copy(
                sections.at[c, :, :, slot], out.at[:, zl, :, c], sem.at[zl, c]
            )
            copy.start()
            copies.append(copy)
    for copy in copies:
        copy.wait()


def split(value):
    high = value.astype(BF16)
    return high, (value - high.astype(F32)).astype(BF16)


def as_left(mat):
    high, low = split(jnp.concatenate(mat, axis=1))
    return jnp.concatenate([high, low], axis=0), high


def as_right(mat):
    real, imag = mat
    real_high, real_low = split(real)
    imag_high, imag_low = split(imag)
    high = jnp.concatenate(
        [
            jnp.concatenate([real_high, imag_high], axis=1),
            jnp.concatenate([-imag_high, real_high], axis=1),
        ],
        axis=0,
    )
    low = jnp.concatenate(
        [
            jnp.concatenate([real_low, imag_low], axis=1),
            jnp.concatenate([-imag_low, real_low], axis=1),
        ],
        axis=0,
    )
    return high, low


def product(outer_mat, inner_mat):
    both, high = as_left(outer_mat)
    right_high, right_low = as_right(inner_mat)
    wide = jnp.dot(both, right_high, preferred_element_type=F32)
    more = jnp.dot(high, right_low, preferred_element_type=F32)
    total = wide[:M] + (wide[M:] + more)
    return total[:, :M], total[:, M:]


def section_of(recv, order, step):
    index = jnp.where(order == 0, step, 15 - step)
    zl, c = index // 4, lax.rem(index, 4)
    return tuple(recv[:, zl, :, c, part].reshape(M, M) for part in range(2))


def tree_kernel(recv, total, keep):
    _, direction, _, _ = place()
    level = [section_of(recv, direction, step) for step in range(16)]
    kept = 0
    while len(level) > 1:
        level = [product(level[2 * k + 1], level[2 * k]) for k in range(len(level) // 2)]
        if len(level) > 1:
            for k in range(0, len(level), 2):
                for part in range(2):
                    keep[kept, part] = level[k][part]
                kept += 1
    for part in range(2):
        total[part] = level[0][part]


def matvec(mat, vec, eye):
    mat_real, mat_imag = mat
    real, imag = vec
    out_real = jnp.sum(mat_real * real - mat_imag * imag, axis=1, keepdims=True)
    out_imag = jnp.sum(mat_real * imag + mat_imag * real, axis=1, keepdims=True)
    return (
        jnp.sum(jnp.where(eye, out_real, 0.0), axis=0, keepdims=True),
        jnp.sum(jnp.where(eye, out_imag, 0.0), axis=0, keepdims=True),
    )


def diagonal():
    return lax.broadcasted_iota(jnp.int32, (M, M), 0) == lax.broadcasted_iota(jnp.int32, (M, M), 1)


def launch_vector(mode, b):
    lane = lax.broadcasted_iota(jnp.int32, (1, M), 1)
    onehot = jnp.where(lane == mode[b], jnp.float32(math.sqrt(M)), 0.0)
    return onehot, jnp.zeros_like(onehot)


def prefix_kernel(recv, keep, total, turned):
    _, direction, _, _ = place()

    def kept(k):
        return keep[k, 0], keep[k, 1]

    def section(step):
        return section_of(recv, direction, step)

    prefix = {1: section(0), 2: kept(0), 4: kept(4), 8: kept(6), 16: (total[0], total[1])}
    prefix[6] = product(kept(1), prefix[4])
    prefix[10] = product(kept(2), prefix[8])
    prefix[12] = product(kept(5), prefix[8])
    prefix[14] = product(kept(3), prefix[12])
    for step in range(2, 16, 2):
        prefix[step + 1] = product(section(step), prefix[step])
    for step in range(1, 17):
        for part in range(2):
            turned[step - 1, part] = prefix[step][part].T


def pair_kernel(own, near, turned, pair):
    del turned
    _, _, spot, _ = place()
    odd = lax.rem(spot, 2) == 1
    first = tuple(jnp.where(odd, near[part], own[part]) for part in range(2))
    second = tuple(jnp.where(odd, own[part], near[part]) for part in range(2))
    result = product(second, first)
    for part in range(2):
        for s in range(4):
            pair[s, part] = result[part]


def fields_kernel(mode, near, mats, turned, out):
    b, direction, spot, upper = place()
    column = 2 * upper + spot // 2
    eye = diagonal()

    def enter(step, vec):
        which = jnp.where(direction == 0, step, 3 - step)
        return matvec((mats[which, 0], mats[which, 1]), vec, eye)

    vec = lax.fori_loop(0, column, enter, launch_vector(mode, b))

    def step_in(step, vec):
        return matvec((near[0], near[1]), vec, eye)

    entering = lax.fori_loop(0, lax.rem(spot, 2), step_in, vec)
    real, imag = (
        jnp.sum(jnp.where(eye, entering[part], 0.0), axis=1, keepdims=True) for part in range(2)
    )
    states = [entering]
    for step in range(16):
        mat_real, mat_imag = turned[step, 0], turned[step, 1]
        states.append(
            (
                jnp.sum(mat_real * real - mat_imag * imag, axis=0, keepdims=True),
                jnp.sum(mat_real * imag + mat_imag * real, axis=0, keepdims=True),
            )
        )
    for index in range(16):
        for part in range(2):
            out[index // 4, 2 * (index % 4) + part : 2 * (index % 4) + part + 1] = jnp.where(
                direction == 0, states[index + 1][part], states[15 - index][part]
            )


def output_kernel(returned, forward, backward):
    zh = lax.axis_index("zh")
    for b in range(2):
        for d, ref in enumerate((forward, backward)):
            block = returned[slot_of(zh, 2 * b + d)]
            for c in range(4):
                ref[c, b] = block[2 * c : 2 * c + 2]


def shards(sections, launch_mode):
    sections = sections.reshape(4, 8, 2, 4, 2, 8, M)
    send = pl.pallas_call(
        gather_kernel,
        out_shape=jax.ShapeDtypeStruct((8, 4, 2, 4, 2, 8, M), F32),
        in_specs=[HBM_SPEC],
        out_specs=VMEM_SPEC,
        scratch_shapes=[pltpu.SemaphoreType.DMA((4, 4))],
        compiler_params=PARAMS,
        name="gather",
    )(sections)
    recv = lax.all_to_all(send.reshape(64, 4, 2, 8, M), ("y", "zl", "core"), 0, 0)
    recv = recv.reshape(8, 4, 2, 4, 2, 8, M)
    total, keep = pl.pallas_call(
        tree_kernel,
        out_shape=(
            jax.ShapeDtypeStruct((2, M, M), F32),
            jax.ShapeDtypeStruct((7, 2, M, M), F32),
        ),
        in_specs=[VMEM_SPEC],
        out_specs=(VMEM_SPEC, VMEM_SPEC),
        compiler_params=PARAMS,
        name="tree",
    )(recv)
    near = lax.ppermute(total, ("zh", "zl"), [(z, 7 - z) for z in range(8)])
    turned = pl.pallas_call(
        prefix_kernel,
        out_shape=jax.ShapeDtypeStruct((16, 2, M, M), F32),
        in_specs=[VMEM_SPEC] * 3,
        out_specs=VMEM_SPEC,
        compiler_params=PARAMS,
        cost_estimate=pl.CostEstimate(
            flops=11 * 6 * 8 * M * M * M, bytes_accessed=6 * 1024 * 1024, transcendentals=0
        ),
        name="prefix",
    )(recv, keep, total)
    pair = pl.pallas_call(
        pair_kernel,
        out_shape=jax.ShapeDtypeStruct((4, 2, M, M), F32),
        in_specs=[VMEM_SPEC] * 3,
        out_specs=VMEM_SPEC,
        compiler_params=PARAMS,
        name="pair",
    )(total, near, turned)
    mats = lax.all_to_all(pair, "x", 0, 0)
    fields = pl.pallas_call(
        fields_kernel,
        out_shape=jax.ShapeDtypeStruct((4, 8, M), F32),
        in_specs=[SMEM_SPEC] + [VMEM_SPEC] * 3,
        out_specs=VMEM_SPEC,
        compiler_params=PARAMS,
        name="fields",
    )(launch_mode, near, mats, turned)
    returned = lax.all_to_all(fields, "zl", 0, 0)
    return pl.pallas_call(
        output_kernel,
        out_shape=(
            jax.ShapeDtypeStruct((4, 2, 2, M), F32),
            jax.ShapeDtypeStruct((4, 2, 2, M), F32),
        ),
        in_specs=[VMEM_SPEC],
        out_specs=(VMEM_SPEC, VMEM_SPEC),
        compiler_params=PARAMS,
        name="outputs",
    )(returned)


def solution(mesh):
    fine = Mesh(mesh.devices.reshape(8, 2, 4, 2, 4), ("y", "core", "x", "zh", "zl"))
    return jax.shard_map(
        shards,
        mesh=fine,
        in_specs=(P(("x", "zh", "zl"), None, None, None, ("y", "core"), None), P(("y", "core"))),
        out_specs=(
            P(("x", "zh", "zl"), ("y", "core"), None, None),
            P(("x", "zh", "zl"), ("y", "core"), None, None),
        ),
        check_vma=False,
    )
```

```python
import math

import jax
import jax.numpy as jnp
from jax import lax
from jax.experimental import pallas as pl
from jax.experimental.pallas import tpu as pltpu
from jax.sharding import Mesh, PartitionSpec as P

M = 128
F32 = jnp.float32
BF16 = jnp.bfloat16
VMEM_SPEC = pl.BlockSpec(memory_space=pltpu.VMEM)
SMEM_SPEC = pl.BlockSpec(memory_space=pltpu.SMEM)
HBM_SPEC = pl.BlockSpec(memory_space=pltpu.HBM)
PARAMS = pltpu.CompilerParams(vmem_limit_bytes=24 * 1024 * 1024)


def slot_of(zh, zl):
    return jnp.where(zh == 0, zl, 3 - zl)


def place():
    x, zh, zl = lax.axis_index("x"), lax.axis_index("zh"), lax.axis_index("zl")
    slot = slot_of(zh, zl)
    direction = lax.rem(slot, 2)
    spot = 2 * x + zh
    spot = jnp.where(direction == 0, spot, 7 - spot)
    return slot // 2, direction, lax.rem(spot, 4), spot // 4


def gather_kernel(sections, out, sem):
    zh = lax.axis_index("zh")
    copies = []
    for zl in range(4):
        slot = slot_of(zh, zl)
        for c in range(4):
            copy = pltpu.make_async_copy(sections.at[c, :, slot], out.at[:, zl, c], sem.at[zl, c])
            copy.start()
            copies.append(copy)
    for copy in copies:
        copy.wait()


def split(value):
    high = value.astype(BF16)
    return high, (value - high.astype(F32)).astype(BF16)


def as_left(mat):
    high, low = split(jnp.concatenate(mat, axis=1))
    return jnp.concatenate([high, low], axis=0), high


def as_right(mat):
    real, imag = mat
    real_high, real_low = split(real)
    imag_high, imag_low = split(imag)
    high = jnp.concatenate(
        [
            jnp.concatenate([real_high, imag_high], axis=1),
            jnp.concatenate([-imag_high, real_high], axis=1),
        ],
        axis=0,
    )
    low = jnp.concatenate(
        [
            jnp.concatenate([real_low, imag_low], axis=1),
            jnp.concatenate([-imag_low, real_low], axis=1),
        ],
        axis=0,
    )
    return high, low


def product(outer_mat, inner_mat):
    both, high = as_left(outer_mat)
    right_high, right_low = as_right(inner_mat)
    wide = jnp.dot(both, right_high, preferred_element_type=F32)
    more = jnp.dot(high, right_low, preferred_element_type=F32)
    total = wide[:M] + (wide[M:] + more)
    return total[:, :M], total[:, M:]


def section_of(recv, order, step):
    index = jnp.where(order == 0, step, 15 - step)
    zl, c = index // 4, lax.rem(index, 4)
    return tuple(recv[:, zl, c, part].reshape(M, M) for part in range(2))


def tree_kernel(recv, total, keep):
    _, direction, _, _ = place()
    level = [section_of(recv, direction, step) for step in range(16)]
    kept = 0
    while len(level) > 1:
        level = [product(level[2 * k + 1], level[2 * k]) for k in range(len(level) // 2)]
        if len(level) > 1:
            for k in range(0, len(level), 2):
                for part in range(2):
                    keep[kept, part] = level[k][part]
                kept += 1
    for part in range(2):
        total[part] = level[0][part]


def matvec(mat, vec, eye):
    mat_real, mat_imag = mat
    real, imag = vec[:2]
    out_real = jnp.sum(mat_real * real - mat_imag * imag, axis=1, keepdims=True)
    out_imag = jnp.sum(mat_real * imag + mat_imag * real, axis=1, keepdims=True)
    return (
        jnp.sum(jnp.where(eye, out_real, 0.0), axis=0, keepdims=True),
        jnp.sum(jnp.where(eye, out_imag, 0.0), axis=0, keepdims=True),
        out_real,
        out_imag,
    )


def diagonal():
    return lax.broadcasted_iota(jnp.int32, (M, M), 0) == lax.broadcasted_iota(jnp.int32, (M, M), 1)


def launch_vector(mode, b):
    forms = []
    for shape, axis in (((1, M), 1), ((M, 1), 0)):
        index = lax.broadcasted_iota(jnp.int32, shape, axis)
        onehot = jnp.where(index == mode[b], jnp.float32(math.sqrt(M)), 0.0)
        forms += [onehot, jnp.zeros_like(onehot)]
    return tuple(forms)


def prefix_kernel(recv, keep, total, turned):
    _, direction, _, _ = place()

    def kept(k):
        return keep[k, 0], keep[k, 1]

    def section(step):
        return section_of(recv, direction, step)

    prefix = {1: section(0), 2: kept(0), 4: kept(4), 8: kept(6), 16: (total[0], total[1])}
    prefix[6] = product(kept(1), prefix[4])
    prefix[10] = product(kept(2), prefix[8])
    prefix[12] = product(kept(5), prefix[8])
    prefix[14] = product(kept(3), prefix[12])
    for step in range(2, 16, 2):
        prefix[step + 1] = product(section(step), prefix[step])
    for step in range(1, 17):
        for part in range(2):
            turned[step - 1, part] = prefix[step][part].T


def pair_kernel(own, near, turned, pair):
    del turned
    _, _, spot, _ = place()
    odd = lax.rem(spot, 2) == 1
    first = tuple(jnp.where(odd, near[part], own[part]) for part in range(2))
    second = tuple(jnp.where(odd, own[part], near[part]) for part in range(2))
    result = product(second, first)
    for part in range(2):
        for s in range(4):
            pair[s, part] = result[part]


def fields_kernel(mode, near, mats, turned, out):
    b, direction, spot, upper = place()
    column = 2 * upper + spot // 2
    eye = diagonal()

    def enter(step, vec):
        which = jnp.where(direction == 0, step, 3 - step)
        return matvec((mats[which, 0], mats[which, 1]), vec, eye)

    vec = lax.fori_loop(0, column, enter, launch_vector(mode, b))

    def step_in(step, vec):
        return matvec((near[0], near[1]), vec, eye)

    entering = lax.fori_loop(0, lax.rem(spot, 2), step_in, vec)
    real, imag = entering[2:]
    states = [entering]
    for step in range(16):
        mat_real, mat_imag = turned[step, 0], turned[step, 1]
        states.append(
            (
                jnp.sum(mat_real * real - mat_imag * imag, axis=0, keepdims=True),
                jnp.sum(mat_real * imag + mat_imag * real, axis=0, keepdims=True),
            )
        )
    for index in range(16):
        for part in range(2):
            out[index // 4, 2 * (index % 4) + part : 2 * (index % 4) + part + 1] = jnp.where(
                direction == 0, states[index + 1][part], states[15 - index][part]
            )


def output_kernel(returned, forward, backward):
    zh = lax.axis_index("zh")
    for b in range(2):
        for d, ref in enumerate((forward, backward)):
            block = returned[slot_of(zh, 2 * b + d)]
            for c in range(4):
                ref[c, b] = block[2 * c : 2 * c + 2]


def shards(sections, launch_mode):
    sections = sections.reshape(4, 16, 4, 2, 8, M)
    send = pl.pallas_call(
        gather_kernel,
        out_shape=jax.ShapeDtypeStruct((16, 4, 4, 2, 8, M), F32),
        in_specs=[HBM_SPEC],
        out_specs=VMEM_SPEC,
        scratch_shapes=[pltpu.SemaphoreType.DMA((4, 4))],
        compiler_params=PARAMS,
        name="gather",
    )(sections)
    recv = lax.all_to_all(send.reshape(64, 4, 2, 8, M), ("y", "core", "zl"), 0, 0)
    recv = recv.reshape(16, 4, 4, 2, 8, M)
    total, keep = pl.pallas_call(
        tree_kernel,
        out_shape=(
            jax.ShapeDtypeStruct((2, M, M), F32),
            jax.ShapeDtypeStruct((7, 2, M, M), F32),
        ),
        in_specs=[VMEM_SPEC],
        out_specs=(VMEM_SPEC, VMEM_SPEC),
        compiler_params=PARAMS,
        name="tree",
    )(recv)
    near = lax.ppermute(total, ("zh", "zl"), [(z, 7 - z) for z in range(8)])
    turned = pl.pallas_call(
        prefix_kernel,
        out_shape=jax.ShapeDtypeStruct((16, 2, M, M), F32),
        in_specs=[VMEM_SPEC] * 3,
        out_specs=VMEM_SPEC,
        compiler_params=PARAMS,
        cost_estimate=pl.CostEstimate(
            flops=11 * 6 * 8 * M * M * M, bytes_accessed=6 * 1024 * 1024, transcendentals=0
        ),
        name="prefix",
    )(recv, keep, total)
    pair = pl.pallas_call(
        pair_kernel,
        out_shape=jax.ShapeDtypeStruct((4, 2, M, M), F32),
        in_specs=[VMEM_SPEC] * 3,
        out_specs=VMEM_SPEC,
        compiler_params=PARAMS,
        name="pair",
    )(total, near, turned)
    mats = lax.all_to_all(pair, "x", 0, 0)
    fields = pl.pallas_call(
        fields_kernel,
        out_shape=jax.ShapeDtypeStruct((4, 8, M), F32),
        in_specs=[SMEM_SPEC] + [VMEM_SPEC] * 3,
        out_specs=VMEM_SPEC,
        compiler_params=PARAMS,
        name="fields",
    )(launch_mode, near, mats, turned)
    returned = lax.all_to_all(fields, "zl", 0, 0)
    return pl.pallas_call(
        output_kernel,
        out_shape=(
            jax.ShapeDtypeStruct((4, 2, 2, M), F32),
            jax.ShapeDtypeStruct((4, 2, 2, M), F32),
        ),
        in_specs=[VMEM_SPEC],
        out_specs=(VMEM_SPEC, VMEM_SPEC),
        compiler_params=PARAMS,
        name="outputs",
    )(returned)


def solution(mesh):
    fine = Mesh(mesh.devices.reshape(8, 2, 4, 2, 4), ("y", "core", "x", "zh", "zl"))
    return jax.shard_map(
        shards,
        mesh=fine,
        in_specs=(P(("x", "zh", "zl"), None, None, None, ("y", "core"), None), P(("y", "core"))),
        out_specs=(
            P(("x", "zh", "zl"), ("y", "core"), None, None),
            P(("x", "zh", "zl"), ("y", "core"), None, None),
        ),
        check_vma=False,
    )
```

```python
import math

import jax
import jax.numpy as jnp
from jax import lax
from jax.experimental import pallas as pl
from jax.experimental.pallas import tpu as pltpu
from jax.sharding import Mesh, PartitionSpec as P

M = 128
F32 = jnp.float32
BF16 = jnp.bfloat16
VMEM_SPEC = pl.BlockSpec(memory_space=pltpu.VMEM)
SMEM_SPEC = pl.BlockSpec(memory_space=pltpu.SMEM)
HBM_SPEC = pl.BlockSpec(memory_space=pltpu.HBM)
PARAMS = pltpu.CompilerParams(vmem_limit_bytes=24 * 1024 * 1024)


def slot_of(zh, zl):
    return jnp.where(zh == 0, zl, 3 - zl)


def place():
    x, zh, zl = lax.axis_index("x"), lax.axis_index("zh"), lax.axis_index("zl")
    slot = slot_of(zh, zl)
    direction = lax.rem(slot, 2)
    spot = 2 * x + zh
    spot = jnp.where(direction == 0, spot, 7 - spot)
    return slot // 2, direction, lax.rem(spot, 4), spot // 4


def gather_kernel(sections, out, sem):
    zh = lax.axis_index("zh")
    copies = []
    for zl in range(4):
        slot = slot_of(zh, zl)
        for c in range(4):
            copy = pltpu.make_async_copy(sections.at[c, :, slot], out.at[:, zl, c], sem.at[zl, c])
            copy.start()
            copies.append(copy)
    for copy in copies:
        copy.wait()


def split(value):
    high = value.astype(BF16)
    return high, (value - high.astype(F32)).astype(BF16)


def as_left(mat):
    high, low = split(jnp.concatenate(mat, axis=1))
    return jnp.concatenate([high, low], axis=0), high


def as_right(mat):
    real, imag = mat
    real_high, real_low = split(real)
    imag_high, imag_low = split(imag)
    high = jnp.concatenate(
        [
            jnp.concatenate([real_high, imag_high], axis=1),
            jnp.concatenate([-imag_high, real_high], axis=1),
        ],
        axis=0,
    )
    low = jnp.concatenate(
        [
            jnp.concatenate([real_low, imag_low], axis=1),
            jnp.concatenate([-imag_low, real_low], axis=1),
        ],
        axis=0,
    )
    return high, low


def product(outer_mat, inner_mat):
    both, high = as_left(outer_mat)
    right_high, right_low = as_right(inner_mat)
    wide = jnp.dot(both, right_high, preferred_element_type=F32)
    more = jnp.dot(high, right_low, preferred_element_type=F32)
    total = wide[:M] + (wide[M:] + more)
    return total[:, :M], total[:, M:]


def section_of(recv, order, step):
    index = jnp.where(order == 0, step, 15 - step)
    zl, c = index // 4, lax.rem(index, 4)
    return tuple(recv[:, zl, c, part].reshape(M, M) for part in range(2))


def tree_kernel(recv, total, keep):
    _, direction, _, _ = place()
    level = [section_of(recv, direction, step) for step in range(16)]
    kept = 0
    while len(level) > 1:
        level = [product(level[2 * k + 1], level[2 * k]) for k in range(len(level) // 2)]
        if len(level) > 1:
            for k in range(0, len(level), 2):
                for part in range(2):
                    keep[kept, part] = level[k][part]
                kept += 1
    for part in range(2):
        total[part] = level[0][part]


def matvec(mat, vec, eye):
    mat_real, mat_imag = mat
    real, imag = vec[:2]
    out_real = jnp.sum(mat_real * real - mat_imag * imag, axis=1, keepdims=True)
    out_imag = jnp.sum(mat_real * imag + mat_imag * real, axis=1, keepdims=True)
    return (
        jnp.sum(jnp.where(eye, out_real, 0.0), axis=0, keepdims=True),
        jnp.sum(jnp.where(eye, out_imag, 0.0), axis=0, keepdims=True),
        out_real,
        out_imag,
    )


def diagonal():
    return lax.broadcasted_iota(jnp.int32, (M, M), 0) == lax.broadcasted_iota(jnp.int32, (M, M), 1)


def launch_vector(mode, b):
    forms = []
    for shape, axis in (((1, M), 1), ((M, 1), 0)):
        index = lax.broadcasted_iota(jnp.int32, shape, axis)
        onehot = jnp.where(index == mode[b], jnp.float32(math.sqrt(M)), 0.0)
        forms += [onehot, jnp.zeros_like(onehot)]
    return tuple(forms)


def prefix_kernel(recv, keep, total, turned):
    _, direction, _, _ = place()

    def kept(k):
        return keep[k, 0], keep[k, 1]

    def section(step):
        return section_of(recv, direction, step)

    prefix = {1: section(0), 2: kept(0), 4: kept(4), 8: kept(6), 16: (total[0], total[1])}
    prefix[6] = product(kept(1), prefix[4])
    prefix[10] = product(kept(2), prefix[8])
    prefix[12] = product(kept(5), prefix[8])
    prefix[14] = product(kept(3), prefix[12])
    for step in range(2, 16, 2):
        prefix[step + 1] = product(section(step), prefix[step])
    eye = jnp.where(diagonal(), 1.0, 0.0)
    prefix[0] = (eye, jnp.zeros_like(eye))
    flat = {step: tuple(part.T for part in prefix[step]) for step in range(17)}
    for index in range(16):
        for part in range(2):
            turned[index, part] = jnp.where(
                direction == 0, flat[index + 1][part], flat[15 - index][part]
            )


def pair_kernel(own, near, turned, pair):
    del turned
    _, _, spot, _ = place()
    odd = lax.rem(spot, 2) == 1
    first = tuple(jnp.where(odd, near[part], own[part]) for part in range(2))
    second = tuple(jnp.where(odd, own[part], near[part]) for part in range(2))
    result = product(second, first)
    for part in range(2):
        for s in range(4):
            pair[s, part] = result[part]


def fields_kernel(mode, near, mats, turned, out):
    b, direction, spot, upper = place()
    column = 2 * upper + spot // 2
    eye = diagonal()

    def enter(step, vec):
        which = jnp.where(direction == 0, step, 3 - step)
        return matvec((mats[which, 0], mats[which, 1]), vec, eye)

    vec = lax.fori_loop(0, column, enter, launch_vector(mode, b))

    def step_in(step, vec):
        return matvec((near[0], near[1]), vec, eye)

    entering = lax.fori_loop(0, lax.rem(spot, 2), step_in, vec)
    real, imag = entering[2:]
    for index in range(16):
        mat_real, mat_imag = turned[index, 0], turned[index, 1]
        row = 2 * (index % 4)
        out[index // 4, row : row + 1] = jnp.sum(
            mat_real * real - mat_imag * imag, axis=0, keepdims=True
        )
        out[index // 4, row + 1 : row + 2] = jnp.sum(
            mat_real * imag + mat_imag * real, axis=0, keepdims=True
        )


def output_kernel(returned, forward, backward):
    zh = lax.axis_index("zh")
    for b in range(2):
        for d, ref in enumerate((forward, backward)):
            block = returned[slot_of(zh, 2 * b + d)]
            for c in range(4):
                ref[c, b] = block[2 * c : 2 * c + 2]


def shards(sections, launch_mode):
    sections = sections.reshape(4, 16, 4, 2, 8, M)
    send = pl.pallas_call(
        gather_kernel,
        out_shape=jax.ShapeDtypeStruct((16, 4, 4, 2, 8, M), F32),
        in_specs=[HBM_SPEC],
        out_specs=VMEM_SPEC,
        scratch_shapes=[pltpu.SemaphoreType.DMA((4, 4))],
        compiler_params=PARAMS,
        name="gather",
    )(sections)
    recv = lax.all_to_all(send.reshape(64, 4, 2, 8, M), ("y", "core", "zl"), 0, 0)
    recv = recv.reshape(16, 4, 4, 2, 8, M)
    total, keep = pl.pallas_call(
        tree_kernel,
        out_shape=(
            jax.ShapeDtypeStruct((2, M, M), F32),
            jax.ShapeDtypeStruct((7, 2, M, M), F32),
        ),
        in_specs=[VMEM_SPEC],
        out_specs=(VMEM_SPEC, VMEM_SPEC),
        compiler_params=PARAMS,
        name="tree",
    )(recv)
    near = lax.ppermute(total, ("zh", "zl"), [(z, 7 - z) for z in range(8)])
    turned = pl.pallas_call(
        prefix_kernel,
        out_shape=jax.ShapeDtypeStruct((16, 2, M, M), F32),
        in_specs=[VMEM_SPEC] * 3,
        out_specs=VMEM_SPEC,
        compiler_params=PARAMS,
        cost_estimate=pl.CostEstimate(
            flops=11 * 6 * 8 * M * M * M, bytes_accessed=6 * 1024 * 1024, transcendentals=0
        ),
        name="prefix",
    )(recv, keep, total)
    pair = pl.pallas_call(
        pair_kernel,
        out_shape=jax.ShapeDtypeStruct((4, 2, M, M), F32),
        in_specs=[VMEM_SPEC] * 3,
        out_specs=VMEM_SPEC,
        compiler_params=PARAMS,
        name="pair",
    )(total, near, turned)
    mats = lax.all_to_all(pair, "x", 0, 0)
    fields = pl.pallas_call(
        fields_kernel,
        out_shape=jax.ShapeDtypeStruct((4, 8, M), F32),
        in_specs=[SMEM_SPEC] + [VMEM_SPEC] * 3,
        out_specs=VMEM_SPEC,
        compiler_params=PARAMS,
        name="fields",
    )(launch_mode, near, mats, turned)
    returned = lax.all_to_all(fields, "zl", 0, 0)
    return pl.pallas_call(
        output_kernel,
        out_shape=(
            jax.ShapeDtypeStruct((4, 2, 2, M), F32),
            jax.ShapeDtypeStruct((4, 2, 2, M), F32),
        ),
        in_specs=[VMEM_SPEC],
        out_specs=(VMEM_SPEC, VMEM_SPEC),
        compiler_params=PARAMS,
        name="outputs",
    )(returned)


def solution(mesh):
    fine = Mesh(mesh.devices.reshape(8, 2, 4, 2, 4), ("y", "core", "x", "zh", "zl"))
    return jax.shard_map(
        shards,
        mesh=fine,
        in_specs=(P(("x", "zh", "zl"), None, None, None, ("y", "core"), None), P(("y", "core"))),
        out_specs=(
            P(("x", "zh", "zl"), ("y", "core"), None, None),
            P(("x", "zh", "zl"), ("y", "core"), None, None),
        ),
        check_vma=False,
    )
```
